512 devices in a mesh: space: 64 (over y, z_hi, core), bead: 8 (over x, z_lo).
Axes of the slice: x: 4, y: 8, z: 8 (z_hi: 4, z_lo: 2; z = z_hi * 2 + z_lo), core: 2. Of those that a mesh axis runs over, the one named last changes fastest.
Arguments:
- positions: float32 [32, 3, 8192], P('bead', None, 'space'), may hold values from 0 to 2
- momenta: float32 [32, 3, 8192], P('bead', None, 'space'), may hold values from -6 to 6
- masses: float32 [8192], P('space'), may hold values from 1 to 4
- features: bfloat16 [32, 8192, 128], P('bead', 'space'), may hold values from -6 to 6
- neighbours: int32 [64, 8192], P(None, 'space'), may hold values from 0 to 383
- images: int32 [64, 8192], P(None, 'space'), may hold values from 0 to 26
- face_map: int32 [2, 64, 128], P(None, 'space'), may hold values from 0 to 127, each once within a row
- w_query: bfloat16 [128, 128], replicated, may hold values from -0.5 to 0.5
- w_key: bfloat16 [128, 128], replicated, may hold values from -0.375 to 0.375
- w_value: bfloat16 [128, 128], replicated, may hold values from -2 to 2
- w_probe: bfloat16 [128, 128], replicated, may hold values from -0.5 to 0.5
- radial_rate: float32 [8], replicated, may hold values from 0.02 to 0.5
Outputs:
- new_positions: float32 [32, 3, 8192], P('bead', None, 'space')
- new_momenta: float32 [32, 3, 8192], P('bead', None, 'space')
The draws below stay inside these ranges and needn't reach their ends.
Inputs may be any that keep to these rules, and one draw needn't show every extreme that they name: `neighbours`: each entry is a row of the atom's slab's extended table: own atoms first, then the ghosts from the lower slab, then those from the upper slab. `face_map`: each row of a slab's block lists every atom of that slab once.
All inputs are finite; a program needn't handle non-finite values.
Results may differ from the reference program's by a relative error of at most 0.0025.
Values may be sent and summed in bfloat16 or wider, within the bound.
No kernel may reach another device: no remote copies, remote signals or barrier semaphores. Data moves between devices by JAX's collectives and lax.ppermute only.
A program may use at most 64 MiB of HBM per device.

```python
import math
import jax
import jax.numpy as jnp
from jax import lax

ATOMS_DEV = 128
CHANNELS = 128
HEADS = 8
NEAR = 64
BEADS = 32
BRICKS = 64
ATOMS = 8192


def touch_ends(result, stream_key, least, largest):
    index_at = [jax.random.randint(jax.random.fold_in(stream_key, axis), (), 0, length) for axis, length in enumerate(result.shape)]
    longest = result.shape.index(max(result.shape))
    next_to = index_at[:longest] + [(index_at[longest] + 1) % result.shape[longest]] + index_at[longest + 1:]
    return result.at[tuple(index_at)].set(least).at[tuple(next_to)].set(largest)


def levels(own_key, dims, pieces, smallest, top_value):
    def one(dim, blocks):
        steps = jax.random.uniform(jax.random.fold_in(jax.random.fold_in(own_key, 6), dim), (blocks,), jnp.float32, smallest / len(pieces), top_value / len(pieces))
        return jnp.repeat(jnp.exp(steps), dims[dim] // blocks).reshape((-1,) + (1,) * (len(dims) - dim - 1))

    gain = one(*pieces[0])
    for cut in pieces[1:]:
        gain = gain * one(*cut)
    return gain


def gaussian(key, dims, scale, reach, shards=(), kind=jnp.bfloat16):
    result = scale * jax.random.normal(key, dims, jnp.float32)
    if shards:
        result = result * levels(key, dims, shards, -0.22, 0.18)
    return jnp.clip(result, -reach, reach).astype(kind)


def setup_inputs(seed: int = 0) -> dict:
    keys = jax.random.split(jax.random.key(seed), 13)
    positions = jnp.clip(2.0 * jax.random.uniform(keys[0], (BEADS, 3, ATOMS), jnp.float32) ** levels(keys[0], (BEADS, 3, ATOMS), ((0, 8), (2, 64)), -0.2, 0.2), 0.0, 2.0)
    momenta = gaussian(keys[1], (BEADS, 3, ATOMS), 1.0, 6.0, ((0, 8), (2, 64)), jnp.float32)
    masses = jnp.clip(jnp.exp(math.log(4.0) - 1.3862944 * jax.random.uniform(keys[2], (ATOMS,), jnp.float32) ** levels(keys[2], (ATOMS,), ((0, 64),), -0.2, 0.2)), 1.0, 4.0)
    features = gaussian(keys[3], (BEADS, ATOMS, CHANNELS), 1.0, 6.0, ((0, 8), (1, 64)))
    neighbours = touch_ends(jax.random.randint(keys[4], (NEAR, ATOMS), 0, 3 * ATOMS_DEV), jax.random.fold_in(keys[4], 1), 0, (3 * ATOMS_DEV) - 1).astype(jnp.int32)
    images = touch_ends(jax.random.randint(keys[5], (NEAR, ATOMS), 0, 27), jax.random.fold_in(keys[5], 1), 0, 26).astype(jnp.int32)
    face_map = jax.vmap(lambda own: jax.random.permutation(own, ATOMS_DEV))(jax.random.split(keys[6], 2 * BRICKS)).reshape((2, BRICKS, ATOMS_DEV)).astype(jnp.int32)
    w_query = gaussian(keys[7], (CHANNELS, CHANNELS), CHANNELS ** -0.5, 0.5)
    w_key = gaussian(keys[8], (CHANNELS, CHANNELS), (2 * CHANNELS) ** -0.5, 0.375)
    w_value = gaussian(keys[9], (CHANNELS, CHANNELS), (CHANNELS // 16) ** -0.5, 2.0)
    w_probe = gaussian(keys[10], (CHANNELS, CHANNELS), CHANNELS ** -0.5, 0.5)
    radial_rate = jnp.clip(jnp.exp(jax.random.uniform(keys[11], (HEADS,), jnp.float32, math.log(0.02), math.log(0.5))), 0.02, 0.5)
    return {"positions": positions, "momenta": momenta, "masses": masses, "features": features, "neighbours": neighbours, "images": images, "face_map": face_map, "w_query": w_query, "w_key": w_key, "w_value": w_value, "w_probe": w_probe, "radial_rate": radial_rate}


STIFFNESS = 1.3
BOX_LENGTH = 2.0
SCORE_CAP = 30.0

def mode_table(bead_count):
    bead_column = jnp.arange(bead_count).astype(jnp.float32)[:, None]
    mode_row = jnp.arange(bead_count).astype(jnp.float32)[None, :]
    mode_index = jnp.arange(bead_count)[None, :] + jnp.zeros((bead_count, 1), jnp.int32)
    angles = 2.0 * jnp.pi * bead_column * mode_row / bead_count
    wave_norm = jnp.sqrt(jnp.float32(2.0 / bead_count))
    flat_norm = jnp.sqrt(jnp.float32(1.0 / bead_count))
    half_count = bead_count // 2
    entries = jnp.where(mode_index < half_count, wave_norm * jnp.cos(angles), wave_norm * jnp.sin(angles))
    entries = jnp.where(mode_index == half_count, flat_norm * jnp.cos(angles), entries)
    entries = jnp.where(mode_index == 0, flat_norm + 0.0 * angles, entries)
    return entries

def frequencies(bead_count):
    mode_float = jnp.arange(bead_count).astype(jnp.float32)
    return 2.0 * STIFFNESS * jnp.sin(jnp.pi * mode_float / bead_count)

def propagate(mode_pos, mode_mom, masses, frequency):
    phase_turn = frequency[:, None, None]
    cosine_turn = jnp.cos(phase_turn)
    sine_turn = jnp.sin(phase_turn)
    safe_turn = jnp.where(phase_turn > 0, phase_turn, 1.0)
    drift_gain = jnp.where(phase_turn > 0, sine_turn / safe_turn, 1.0)
    mass_row = masses[None, None, :]
    next_pos = cosine_turn * mode_pos + drift_gain * mode_mom / mass_row
    next_mom = cosine_turn * mode_mom - mass_row * phase_turn * sine_turn * mode_pos
    return (next_pos, next_mom)

def image_offsets(images):
    offset_x = images % 3 - 1
    offset_y = images // 3 % 3 - 1
    offset_z = images // 9 - 1
    return BOX_LENGTH * jnp.stack([offset_x, offset_y, offset_z]).astype(jnp.float32)

def probe_matrices(own_features, w_query, w_key, w_value, w_probe, head_count):
    atom_count, channels = own_features.shape
    head_size = channels // head_count
    queries = jnp.dot(own_features, w_query, preferred_element_type=jnp.float32).reshape(atom_count, head_count, head_size)
    probes = jnp.dot(own_features, w_probe, preferred_element_type=jnp.float32).reshape(atom_count, head_count, head_size)
    key_heads = w_key.astype(jnp.float32).reshape(channels, head_count, head_size)
    value_heads = w_value.astype(jnp.float32).reshape(channels, head_count, head_size)
    key_probe = jnp.einsum('ahd,chd->ahc', queries, key_heads, precision=lax.Precision.HIGHEST)
    value_probe = jnp.einsum('ahd,chd->ahc', probes, value_heads, precision=lax.Precision.HIGHEST)
    return jnp.concatenate([key_probe, value_probe], axis=1).astype(jnp.bfloat16)

def attend_forces(pair_terms, offsets, radial_rate, head_size):
    head_count = radial_rate.shape[0]
    scores = pair_terms[:head_count] * head_size ** (-0.5)
    capped = SCORE_CAP * jnp.tanh(scores / SCORE_CAP)
    distance = lax.optimization_barrier(jnp.sum(offsets * offsets, axis=0))
    logits = capped - radial_rate[:, None, None] * distance[None]
    weights = jnp.exp(logits)
    attention = weights / lax.optimization_barrier(jnp.sum(weights, axis=1, keepdims=True))
    coupling = lax.optimization_barrier(jnp.sum(attention * pair_terms[head_count:], axis=0)) * (1.0 / (head_count * head_size ** 0.5))
    return lax.optimization_barrier(jnp.sum(coupling[None] * offsets, axis=1))

def brick_forces(feature_table, coordinate_table, neighbours, images, w_query, w_key, w_value, w_probe, radial_rate):
    atom_count = neighbours.shape[1]
    head_count = radial_rate.shape[0]
    head_size = feature_table.shape[1] // head_count
    probe_mats = probe_matrices(feature_table[:atom_count], w_query, w_key, w_value, w_probe, head_count)
    gathered = feature_table[neighbours]
    offsets = coordinate_table[:, neighbours] - coordinate_table[:, :atom_count][:, None, :] + image_offsets(images)
    pair_terms = jnp.einsum('kac,aec->eka', gathered.astype(jnp.float32), probe_mats.astype(jnp.float32))
    return attend_forces(pair_terms, offsets, radial_rate, head_size)

def reference(positions, momenta, masses, features, neighbours, images, face_map, w_query, w_key, w_value, w_probe, radial_rate):
    bead_count = positions.shape[0]
    brick_count = face_map.shape[1]
    atom_count = face_map.shape[2]
    channels = features.shape[2]
    near_count = neighbours.shape[0]
    feature_blocks = features.reshape(bead_count, brick_count, atom_count, channels)
    coordinate_blocks = positions.reshape(bead_count, 3, brick_count, atom_count).transpose(0, 2, 1, 3)
    from_lower = jnp.roll(face_map[1], 1, axis=0)
    from_upper = jnp.roll(face_map[0], -1, axis=0)
    lower_features = jnp.take_along_axis(jnp.roll(feature_blocks, 1, axis=1), from_lower[None, :, :, None], axis=2)
    upper_features = jnp.take_along_axis(jnp.roll(feature_blocks, -1, axis=1), from_upper[None, :, :, None], axis=2)
    lower_coords = jnp.take_along_axis(jnp.roll(coordinate_blocks, 1, axis=1), from_lower[None, :, None, :], axis=3)
    upper_coords = jnp.take_along_axis(jnp.roll(coordinate_blocks, -1, axis=1), from_upper[None, :, None, :], axis=3)
    feature_tables = jnp.concatenate([feature_blocks, lower_features, upper_features], axis=2)
    coordinate_tables = jnp.concatenate([coordinate_blocks, lower_coords, upper_coords], axis=3)
    brick_neighbours = neighbours.reshape(near_count, brick_count, atom_count).transpose(1, 0, 2)
    brick_images = images.reshape(near_count, brick_count, atom_count).transpose(1, 0, 2)

    def per_brick(items):
        return brick_forces(items[0], items[1], items[2], items[3], w_query, w_key, w_value, w_probe, radial_rate)

    def per_bead(items):
        return lax.map(per_brick, (items[0], items[1], brick_neighbours, brick_images))
    forces = lax.map(per_bead, (feature_tables, coordinate_tables))
    forces = forces.transpose(0, 2, 1, 3).reshape(bead_count, 3, brick_count * atom_count)
    kicked = momenta + forces
    transform = mode_table(bead_count)
    frequency = frequencies(bead_count)
    mode_pos = jnp.einsum('bk,bcn->kcn', transform, positions, precision=lax.Precision.HIGHEST)
    mode_mom = jnp.einsum('bk,bcn->kcn', transform, kicked, precision=lax.Precision.HIGHEST)
    next_pos, next_mom = propagate(mode_pos, mode_mom, masses, frequency)
    new_positions = jnp.einsum('bk,kcn->bcn', transform, next_pos, precision=lax.Precision.HIGHEST)
    new_momenta = jnp.einsum('bk,kcn->bcn', transform, next_mom, precision=lax.Precision.HIGHEST)
    return (new_positions, new_momenta)
```

```python
import jax
import jax.numpy as jnp
import numpy as np
from jax import lax
from jax.experimental import pallas as pl
from jax.experimental.pallas import tpu as pltpu
from jax.sharding import PartitionSpec as P

STIFFNESS = 1.3
BOX_LENGTH = 2.0
SCORE_CAP = 30.0
HEADS = 8
EXTRA = 16

F32 = jnp.float32
BF16 = jnp.bfloat16
NT = (((1,), (1,)), ((), ()))
NN = (((1,), (0,)), ((), ()))


def dot(a, b, dims=NN):
    return lax.dot_general(a, b, dims, preferred_element_type=F32)


def halves(x):
    high = x.astype(BF16)
    low = (x - high.astype(F32)).astype(BF16)
    return high, low


def bead_maps(bead_count, groups):
    bead = np.arange(bead_count, dtype=np.float64)[:, None]
    mode = np.arange(bead_count)[None, :]
    angle = 2.0 * np.pi * bead * mode / bead_count
    wave = np.sqrt(2.0 / bead_count)
    flat = np.sqrt(1.0 / bead_count)
    half = bead_count // 2
    table = np.where(mode < half, wave * np.cos(angle), wave * np.sin(angle))
    table = np.where(mode == half, flat * np.cos(angle), table)
    table = np.where(mode == 0, flat, table)
    turn = 2.0 * STIFFNESS * np.sin(np.pi * np.arange(bead_count) / bead_count)
    gain = np.where(turn > 0, np.sin(turn) / np.where(turn > 0, turn, 1.0), 1.0)
    keep = (table * np.cos(turn)) @ table.T
    drift = (table * gain) @ table.T
    pull = (table * (turn * np.sin(turn))) @ table.T
    local = bead_count // groups

    def rows(m):
        return m.reshape(groups, local, bead_count)

    of_pos = np.concatenate([rows(keep), rows(pull)], axis=1)
    of_mom = np.concatenate([rows(drift), rows(keep)], axis=1)
    return np.stack([of_pos, of_mom], axis=1).astype(np.float32)


def pack_kernel(features, positions, face_map, out):
    beads, atoms, _ = features.shape
    for b in range(beads):
        out[b, :atoms, :] = features[b]
        p = positions[:, b, :]
        high = p.astype(BF16)
        rest = p - high.astype(F32)
        mid = rest.astype(BF16)
        low = (rest - mid.astype(F32)).astype(BF16)
        maps = jnp.concatenate([face_map[0], face_map[1]], axis=0).astype(F32).astype(BF16)
        fill = jnp.zeros((EXTRA - 11, atoms), BF16)
        out[b, atoms:, :] = jnp.concatenate([high, mid, low, maps, fill], axis=0)


def pair_lanes(a, b):
    lane = lax.broadcasted_iota(jnp.int32, a.shape, 1)
    return jnp.where(lane < a.shape[1] // 2, a, b)


def lanes_of(x, index):
    return jnp.take_along_axis(x, index, axis=1, mode="promise_in_bounds")


def doubled(x):
    return jnp.concatenate([x, x], axis=0).T


def own_kernel(features, neighbours, w_query, w_key, w_value, w_probe, probes, values, kp):
    beads, atoms, channels = features.shape
    head_size = channels // HEADS
    x = features[...].reshape(beads * atoms, channels)
    lane = lax.broadcasted_iota(jnp.int32, (channels, channels), 1)
    for which, (w_in, w_out) in enumerate(((w_query, w_key), (w_probe, w_value))):
        q = dot(x, w_in[...])
        q_high, q_low = halves(q)
        q2 = jnp.concatenate([q_high, q_low], axis=1)
        w = w_out[...]
        for h in range(0, HEADS, 2):
            w0 = jnp.where(lane // head_size == h, w, jnp.zeros_like(w))
            w1 = jnp.where(lane // head_size == h + 1, w, jnp.zeros_like(w))
            rhs = jnp.concatenate(
                [jnp.concatenate([w0, w0], axis=1), jnp.concatenate([w1, w1], axis=1)], axis=0
            )
            r = dot(q2, rhs, NT).astype(BF16).reshape(beads, atoms, 2 * channels)
            e = which * HEADS + h
            probes[:, e] = r[:, :, :channels]
            probes[:, e + 1] = r[:, :, channels:]
    index = doubled(neighbours[...]) & (atoms - 1)
    for b in range(beads):
        own = features[b]
        for p in range(HEADS // 2):
            for which in range(2):
                e = which * HEADS + p
                s0 = dot(probes[b, e], own, NT)
                s1 = dot(probes[b, e + HEADS // 2], own, NT)
                values[b, p * 2 + which] = pair_lanes(lanes_of(s0, index), lanes_of(s1, index))


def whole(piece, atoms, b, c):
    r = piece[b, atoms:, :].astype(F32)
    return r[c : c + 1] + r[3 + c : 4 + c] + r[6 + c : 7 + c]


def force_kernel(
    lower, upper, probes, values, neighbours, images, positions, momenta, rate, out
):
    beads = lower.shape[0]
    atoms, channels = probes.shape[2], probes.shape[3]
    head_size = channels // HEADS
    near2 = doubled(neighbours[...])
    image = doubled(images[...])
    slab = near2 // atoms
    index = near2 & (atoms - 1)
    low_map = lower[0, atoms + 10 : atoms + 11, :].astype(F32).astype(jnp.int32)
    up_map = upper[0, atoms + 9 : atoms + 10, :].astype(F32).astype(jnp.int32)
    index_low = lanes_of(jnp.broadcast_to(low_map, index.shape), index)
    index_up = lanes_of(jnp.broadcast_to(up_map, index.shape), index)
    is_own = slab == 0
    is_low = slab == 1
    shift = [
        BOX_LENGTH * (m - 1).astype(F32) for m in (image % 3, image // 3 % 3, image // 9)
    ]
    row = lax.broadcasted_iota(jnp.int32, (atoms, atoms), 0)
    col = lax.broadcasted_iota(jnp.int32, (atoms, atoms), 1)
    half = atoms // 2
    same_half = jnp.where((row < half) == (col < half), 1.0, 0.0).astype(BF16)
    same_half2 = jnp.concatenate([same_half, same_half], axis=0)
    ones = jnp.ones((8, 2 * atoms), BF16)
    lane = lax.broadcasted_iota(jnp.int32, (1, atoms), 1)

    def one_bead(b):
        ghosts = jnp.concatenate([lower[b, :atoms, :], upper[b, :atoms, :]], axis=0)
        offsets = []
        for c in range(3):
            own_row = positions[c, b : b + 1, :]
            near_pos = jnp.where(
                is_own,
                lanes_of(jnp.broadcast_to(own_row, index.shape), index),
                jnp.where(
                    is_low,
                    lanes_of(jnp.broadcast_to(whole(lower, atoms, b, c), index.shape), index_low),
                    lanes_of(jnp.broadcast_to(whole(upper, atoms, b, c), index.shape), index_up),
                ),
            )
            own_col = jnp.broadcast_to(own_row, (atoms, atoms)).T
            offsets.append(near_pos - own_col + shift[c])
        dist = offsets[0] * offsets[0] + offsets[1] * offsets[1] + offsets[2] * offsets[2]

        def slot_values(e, own_value):
            s0 = dot(probes[b, e], ghosts, NT)
            s1 = dot(probes[b, e + HEADS // 2], ghosts, NT)
            from_low = pair_lanes(lanes_of(s0[:, :atoms], index_low), lanes_of(s1[:, :atoms], index_low))
            from_up = pair_lanes(lanes_of(s0[:, atoms:], index_up), lanes_of(s1[:, atoms:], index_up))
            return jnp.where(is_own, own_value, jnp.where(is_low, from_low, from_up))

        total = jnp.zeros((atoms, atoms), F32)
        for p in range(HEADS // 2):
            raw = slot_values(p, values[b, 2 * p])
            strength = slot_values(HEADS + p, values[b, 2 * p + 1])
            rates = jnp.where(lane < half, rate[0, p], rate[0, p + HEADS // 2])
            logit = SCORE_CAP * jnp.tanh(raw * (head_size**-0.5 / SCORE_CAP)) - rates * dist
            weight = jnp.exp(logit)
            w_high, w_low = halves(weight)
            norm = dot(jnp.concatenate([w_high, w_low], axis=1), same_half2)
            total = total + weight / norm * strength
        total = total * (1.0 / (HEADS * head_size**0.5))
        for c in range(3):
            f_high, f_low = halves(total * offsets[c])
            f = dot(ones, jnp.concatenate([f_high, f_low], axis=1), NT)[0:1]
            kicked = momenta[c, b : b + 1, :] + f
            for g in range(out.shape[0]):
                out[g, 1, c, b : b + 1, :] = kicked
                out[g, 0, c, b : b + 1, :] = positions[c, b : b + 1, :]

    for b in range(beads):
        one_bead(b)


def bead_kernel(group, everyone, masses, table, new_pos, new_mom):
    groups, _, _, local, atoms = everyone.shape
    g = group[0]
    of_pos = table[g, 0]
    of_mom = table[g, 1]
    m = masses[...]
    for c in range(3):
        pos = everyone[:, 0, c].reshape(groups * local, atoms)
        mom = everyone[:, 1, c].reshape(groups * local, atoms)
        a = lax.dot_general(of_pos, pos, NN, precision=lax.Precision.HIGHEST, preferred_element_type=F32)
        d = lax.dot_general(of_mom, mom, NN, precision=lax.Precision.HIGHEST, preferred_element_type=F32)
        new_pos[c] = a[:local] + d[:local] / m
        new_mom[c] = d[local:] - m * a[local:]


def vmem(n):
    return [pl.BlockSpec(memory_space=pltpu.VMEM)] * n


SMEM_SPEC = pl.BlockSpec(memory_space=pltpu.SMEM)


def pack(features, positions, face_map):
    beads, atoms, channels = features.shape
    return pl.pallas_call(
        pack_kernel,
        out_shape=jax.ShapeDtypeStruct((beads, atoms + EXTRA, channels), BF16),
        in_specs=vmem(3),
        out_specs=vmem(1)[0],
        name="pack",
    )(features, positions, face_map)


def own_slab(features, neighbours, w_query, w_key, w_value, w_probe):
    beads, atoms, channels = features.shape
    return pl.pallas_call(
        lambda *refs: own_kernel(*refs, None),
        out_shape=(
            jax.ShapeDtypeStruct((beads, 2 * HEADS, atoms, channels), BF16),
            jax.ShapeDtypeStruct((beads, HEADS, atoms, atoms), F32),
        ),
        in_specs=vmem(6),
        out_specs=tuple(vmem(2)),
        name="own_slab",
    )(features, neighbours, w_query, w_key, w_value, w_probe)


def forces(groups, lower, upper, probes, values, neighbours, images, positions, momenta, rate):
    beads = lower.shape[0]
    atoms = probes.shape[2]
    return pl.pallas_call(
        force_kernel,
        out_shape=jax.ShapeDtypeStruct((groups, 2, 3, beads, atoms), F32),
        in_specs=vmem(8) + [SMEM_SPEC],
        out_specs=vmem(1)[0],
        name="forces",
    )(lower, upper, probes, values, neighbours, images, positions, momenta, rate)


def move_beads(group, everyone, masses, table):
    _, _, _, local, atoms = everyone.shape
    return pl.pallas_call(
        bead_kernel,
        out_shape=(jax.ShapeDtypeStruct((3, local, atoms), F32),) * 2,
        in_specs=[SMEM_SPEC] + vmem(3),
        out_specs=tuple(vmem(2)),
        name="bead_maps",
    )(group, everyone, masses, table)


def body(
    positions, momenta, masses, features, neighbours, images, face_map,
    w_query, w_key, w_value, w_probe, radial_rate,
):
    groups = lax.axis_size("bead")
    beads = positions.shape[0]
    slabs = lax.axis_size("space")
    up = [(i, (i + 1) % slabs) for i in range(slabs)]
    down = [(target, source) for source, target in up]
    pos = jnp.transpose(positions, (1, 0, 2))
    mom = jnp.transpose(momenta, (1, 0, 2))
    message = pack(features, pos, face_map)
    lower = lax.ppermute(message, "space", up)
    upper = lax.ppermute(message, "space", down)
    probes, values = own_slab(features, neighbours, w_query, w_key, w_value, w_probe)
    sent = forces(
        groups, lower, upper, probes, values, neighbours, images, pos, mom, radial_rate[None]
    )
    everyone = lax.all_to_all(sent, "bead", 0, 0, tiled=True)
    table = jnp.asarray(bead_maps(beads * groups, groups))
    group = lax.axis_index("bead").astype(jnp.int32)[None]
    new_pos, new_mom = move_beads(group, everyone, masses[None], table)
    return jnp.transpose(new_pos, (1, 0, 2)), jnp.transpose(new_mom, (1, 0, 2))


def solution(mesh):
    placed = (
        P("bead", None, "space"),
        P("bead", None, "space"),
        P("space"),
        P("bead", "space", None),
        P(None, "space"),
        P(None, "space"),
        P(None, "space", None),
        P(), P(), P(), P(), P(),
    )
    return jax.shard_map(
        body,
        mesh=mesh,
        in_specs=placed,
        out_specs=(P("bead", None, "space"), P("bead", None, "space")),
        check_vma=False,
    )
```

```python
import jax
import jax.numpy as jnp
import numpy as np
from jax import lax
from jax.experimental import pallas as pl
from jax.experimental.pallas import tpu as pltpu
from jax.sharding import PartitionSpec as P

STIFFNESS = 1.3
BOX_LENGTH = 2.0
SCORE_CAP = 30.0
HEADS = 8
EXTRA = 16
ROWS = 16
STEP = 128
SCOPE = 24 << 20

F32 = jnp.float32
BF16 = jnp.bfloat16
NT = (((1,), (1,)), ((), ()))
NN = (((1,), (0,)), ((), ()))


def dot(a, b, dims=NN):
    return lax.dot_general(a, b, dims, preferred_element_type=F32)


def halves(x):
    high = x.astype(BF16)
    low = (x - high.astype(F32)).astype(BF16)
    return high, low


def bead_maps(bead_count, groups):
    bead = np.arange(bead_count, dtype=np.float64)[:, None]
    mode = np.arange(bead_count)[None, :]
    angle = 2.0 * np.pi * bead * mode / bead_count
    wave = np.sqrt(2.0 / bead_count)
    flat = np.sqrt(1.0 / bead_count)
    half = bead_count // 2
    table = np.where(mode < half, wave * np.cos(angle), wave * np.sin(angle))
    table = np.where(mode == half, flat * np.cos(angle), table)
    table = np.where(mode == 0, flat, table)
    turn = 2.0 * STIFFNESS * np.sin(np.pi * np.arange(bead_count) / bead_count)
    gain = np.where(turn > 0, np.sin(turn) / np.where(turn > 0, turn, 1.0), 1.0)
    keep = (table * np.cos(turn)) @ table.T
    drift = (table * gain) @ table.T
    pull = (table * (turn * np.sin(turn))) @ table.T
    local = bead_count // groups

    def rows(m):
        return m.reshape(groups, local, bead_count)

    of_pos = np.concatenate([rows(keep), rows(pull)], axis=1)
    of_mom = np.concatenate([rows(drift), rows(keep)], axis=1)
    return np.stack([of_pos, of_mom], axis=1).astype(np.float32)


def pack_kernel(features, positions, face_map, out):
    beads, atoms, _ = features.shape
    for b in range(beads):
        out[b, :atoms, :] = features[b]
        p = positions[:, b, :]
        high = p.astype(BF16)
        rest = p - high.astype(F32)
        mid = rest.astype(BF16)
        low = (rest - mid.astype(F32)).astype(BF16)
        maps = jnp.concatenate([face_map[0], face_map[1]], axis=0).astype(F32).astype(BF16)
        fill = jnp.zeros((EXTRA - 11, atoms), BF16)
        out[b, atoms:, :] = jnp.concatenate([high, mid, low, maps, fill], axis=0)


def pair_lanes(a, b):
    lane = lax.broadcasted_iota(jnp.int32, a.shape, 1)
    return jnp.where(lane < a.shape[1] // 2, a, b)


def lanes_of(x, index):
    return jnp.take_along_axis(x, index, axis=1, mode="promise_in_bounds")


def doubled(x):
    return jnp.concatenate([x, x], axis=0).T


def own_kernel(
    features, neighbours, images, positions, w_query, w_key, w_value, w_probe,
    probes, values, base, near,
):
    beads, atoms, channels = features.shape
    head_size = channels // HEADS
    x = features[...].reshape(beads * atoms, channels)
    lane = lax.broadcasted_iota(jnp.int32, (channels, channels), 1)
    for which, (w_in, w_out) in enumerate(((w_query, w_key), (w_probe, w_value))):
        q = dot(x, w_in[...])
        q_high, q_low = halves(q)
        q2 = jnp.concatenate([q_high, q_low], axis=1)
        w = w_out[...]
        for h in range(0, HEADS, 2):
            w0 = jnp.where(lane // head_size == h, w, jnp.zeros_like(w))
            w1 = jnp.where(lane // head_size == h + 1, w, jnp.zeros_like(w))
            rhs = jnp.concatenate(
                [jnp.concatenate([w0, w0], axis=1), jnp.concatenate([w1, w1], axis=1)], axis=0
            )
            r = dot(q2, rhs, NT).astype(BF16).reshape(beads, atoms // ROWS, ROWS, 2 * channels)
            at = (which * HEADS + h) * ROWS
            probes[:, :, at : at + ROWS, :] = r[..., :channels]
            probes[:, :, at + ROWS : at + 2 * ROWS, :] = r[..., channels:]
    near2 = doubled(neighbours[...])
    near[...] = near2
    is_own = near2 < atoms
    index = near2 & (atoms - 1)
    image = images[...]
    plane = lax.div(image, 9)
    rest = image - 9 * plane
    line = lax.div(rest, 3)
    shift = [
        doubled(BOX_LENGTH * (m - 1).astype(F32)) for m in (rest - 3 * line, line, plane)
    ]
    for b in range(beads):
        own = features[b]
        rows = [positions[c, b : b + 1, :] for c in range(3)]
        wide = [jnp.broadcast_to(r, (8, atoms)) for r in rows]
        cols = [jnp.broadcast_to(r, (atoms, atoms)).T for r in rows]
        for g in range(atoms // ROWS):
            s = dot(probes[b, g], own, NT)
            for half in range(0, ROWS, 8):
                lo = g * ROWS + half
                idx = index[lo : lo + 8]
                got = [lanes_of(s[e * ROWS + half : e * ROWS + half + 8], idx) for e in range(2 * HEADS)]
                here = [lanes_of(wide[c], idx) for c in range(3)]
                for p in range(HEADS // 2):
                    for which in range(2):
                        e = which * HEADS + p
                        values[b, 2 * p + which, lo : lo + 8, :] = pair_lanes(got[e], got[e + HEADS // 2])
                for c in range(3):
                    base[b, c, lo : lo + 8, :] = (
                        jnp.where(is_own[lo : lo + 8], here[c], 0.0)
                        - cols[c][lo : lo + 8]
                        + shift[c][lo : lo + 8]
                    )


def whole(piece, atoms, b):
    r = piece[b, atoms:, :].astype(F32)
    return [
        jnp.broadcast_to(r[c : c + 1] + r[3 + c : 4 + c] + r[6 + c : 7 + c], (8, r.shape[1]))
        for c in range(3)
    ]


def force_kernel(
    lower, upper, probes, values, base, near, positions, momenta, rate, out,
    weights, products, forces, raw_scores, picked, indices,
):
    beads = lower.shape[0]
    atoms = values.shape[2]
    channels = probes.shape[3]
    head_size = channels // HEADS
    pairs = HEADS // 2
    near2 = near[...]
    index = near2 & (atoms - 1)
    low_map = lower[0, atoms + 10 : atoms + 11, :].astype(F32).astype(jnp.int32)
    up_map = upper[0, atoms + 9 : atoms + 10, :].astype(F32).astype(jnp.int32)
    indices[0] = lanes_of(jnp.broadcast_to(low_map, index.shape), index)
    indices[1] = lanes_of(jnp.broadcast_to(up_map, index.shape), index)
    row = lax.broadcasted_iota(jnp.int32, (atoms, atoms), 0)
    col = lax.broadcasted_iota(jnp.int32, (atoms, atoms), 1)
    half_lanes = atoms // 2
    same_half = jnp.where((row < half_lanes) == (col < half_lanes), 1.0, 0.0).astype(BF16)
    same_half2 = jnp.concatenate([same_half, same_half], axis=0)
    ones = jnp.ones((8, 2 * atoms), BF16)
    lane = lax.broadcasted_iota(jnp.int32, (8, atoms), 1)
    rates = [jnp.where(lane < half_lanes, rate[0, p], rate[0, p + pairs]) for p in range(pairs)]

    blocks = atoms // STEP
    steps = beads * blocks
    offs = range(0, STEP, 8)

    def scores(i):
        b, q = lax.div(i, blocks), lax.rem(i, blocks)
        ghosts = jnp.concatenate([lower[b, :atoms, :], upper[b, :atoms, :]], axis=0)
        for k in range(STEP // ROWS):
            raw_scores[k] = dot(probes[b, q * (STEP // ROWS) + k], ghosts, NT)

    def select(i):
        b, q = lax.div(i, blocks), lax.rem(i, blocks)
        pos_low = whole(lower, atoms, b)
        pos_up = whole(upper, atoms, b)
        for lo in offs:
            k, half = lo // ROWS, lo % ROWS
            rows = pl.ds(pl.multiple_of(q * STEP + lo, 8), 8)
            n = near[rows, :]
            is_own = n < atoms
            is_low = n < 2 * atoms
            idx_low = indices[0, rows, :]
            idx_up = indices[1, rows, :]
            at = [slice(e * ROWS + half, e * ROWS + half + 8) for e in range(2 * HEADS)]
            from_low = [lanes_of(raw_scores[k, a, :atoms], idx_low) for a in at]
            p_low = [lanes_of(x, idx_low) for x in pos_low]
            from_up = [lanes_of(raw_scores[k, a, atoms:], idx_up) for a in at]
            p_up = [lanes_of(x, idx_up) for x in pos_up]
            ghost = [jnp.where(is_low, l, u) for l, u in zip(from_low, from_up)]
            for c in range(3):
                off = base[b, c, rows, :] + jnp.where(
                    is_own, 0.0, jnp.where(is_low, p_low[c], p_up[c])
                )
                picked[HEADS + c, lo : lo + 8, :] = off
            for which in range(2):
                for p in range(pairs):
                    e = which * HEADS + p
                    picked[2 * p + which, lo : lo + 8, :] = jnp.where(
                        is_own,
                        values[b, 2 * p + which, rows, :],
                        pair_lanes(ghost[e], ghost[e + pairs]),
                    )

    def weigh(i):
        b, q = lax.div(i, blocks), lax.rem(i, blocks)
        whole_block = pl.ds(pl.multiple_of(q * STEP, 8), STEP)
        total = None
        for p in range(pairs):
            for lo in offs:
                here = slice(lo, lo + 8)
                off = [picked[HEADS + c, here, :] for c in range(3)]
                dist = off[0] * off[0] + off[1] * off[1] + off[2] * off[2]
                logit = (
                    SCORE_CAP * jnp.tanh(picked[2 * p, here, :] * (head_size**-0.5 / SCORE_CAP))
                    - rates[p] * dist
                )
                weight = jnp.exp(logit)
                products[p, here, :] = weight * picked[2 * p + 1, here, :]
                weights[p, here, :] = weight
            w_high, w_low = halves(weights[p])
            norm = dot(jnp.concatenate([w_high, w_low], axis=1), same_half2)
            part = products[p] / norm
            total = part if total is None else total + part
        total = total * (1.0 / (HEADS * head_size**0.5))
        for c in range(3):
            forces[b, c, whole_block, :] = total * picked[HEADS + c]

    def finish(b):
        for c in range(3):
            f_high, f_low = halves(forces[b, c])
            f = dot(ones, jnp.concatenate([f_high, f_low], axis=1), NT)[0:1]
            kicked = momenta[c, b : b + 1, :] + f
            for g in range(out.shape[0]):
                out[g, 1, c, b : b + 1, :] = kicked
                out[g, 0, c, b : b + 1, :] = positions[c, b : b + 1, :]

    scores(0)
    select(0)
    scores(1)

    def step(i, carry):
        weigh(i)
        select(i + 1)
        scores(i + 2)
        return carry

    lax.fori_loop(0, steps - 2, step, 0)
    weigh(steps - 2)
    select(steps - 1)
    weigh(steps - 1)
    for b in range(beads):
        finish(b)


def bead_kernel(group, everyone, masses, table, new_pos, new_mom):
    groups, _, _, local, atoms = everyone.shape
    g = group[0]
    of_pos = table[g, 0]
    of_mom = table[g, 1]
    m = masses[...]
    for c in range(3):
        pos = everyone[:, 0, c].reshape(groups * local, atoms)
        mom = everyone[:, 1, c].reshape(groups * local, atoms)
        a = lax.dot_general(of_pos, pos, NN, precision=lax.Precision.HIGHEST, preferred_element_type=F32)
        d = lax.dot_general(of_mom, mom, NN, precision=lax.Precision.HIGHEST, preferred_element_type=F32)
        new_pos[c] = a[:local] + d[:local] / m
        new_mom[c] = d[local:] - m * a[local:]


def vmem(n):
    return [pl.BlockSpec(memory_space=pltpu.VMEM)] * n


SMEM_SPEC = pl.BlockSpec(memory_space=pltpu.SMEM)


def inside(x):
    return pltpu.with_memory_space_constraint(x, pltpu.VMEM)


def outside(x):
    return pltpu.with_memory_space_constraint(x, pltpu.HBM)


def pack(features, positions, face_map):
    beads, atoms, channels = features.shape
    return pl.pallas_call(
        pack_kernel,
        out_shape=pltpu.VMEM((beads, atoms + EXTRA, channels), BF16),
        in_specs=vmem(3),
        out_specs=vmem(1)[0],
        compiler_params=pltpu.CompilerParams(vmem_limit_bytes=SCOPE),
        name="pack",
    )(features, positions, face_map)


def own_slab(features, neighbours, images, positions, *weights):
    beads, atoms, channels = features.shape
    return pl.pallas_call(
        own_kernel,
        out_shape=(
            pltpu.VMEM((beads, atoms // ROWS, 2 * HEADS * ROWS, channels), BF16),
            pltpu.VMEM((beads, HEADS, atoms, atoms), F32),
            pltpu.VMEM((beads, 3, atoms, atoms), F32),
            pltpu.VMEM((atoms, atoms), jnp.int32),
        ),
        in_specs=vmem(8),
        out_specs=tuple(vmem(4)),
        compiler_params=pltpu.CompilerParams(vmem_limit_bytes=SCOPE),
        name="own_slab",
    )(features, neighbours, images, positions, *weights)


def forces(groups, lower, upper, probes, values, base, near, positions, momenta, rate):
    beads = lower.shape[0]
    atoms = values.shape[2]
    return pl.pallas_call(
        force_kernel,
        out_shape=jax.ShapeDtypeStruct((groups, 2, 3, beads, atoms), F32),
        in_specs=vmem(8) + [SMEM_SPEC],
        out_specs=vmem(1)[0],
        scratch_shapes=[
            pltpu.VMEM((HEADS // 2, STEP, atoms), F32),
            pltpu.VMEM((HEADS // 2, STEP, atoms), F32),
            pltpu.VMEM((beads, 3, atoms, atoms), F32),
            pltpu.VMEM((STEP // ROWS, 2 * HEADS * ROWS, 2 * atoms), F32),
            pltpu.VMEM((HEADS + 3, STEP, atoms), F32),
            pltpu.VMEM((2, atoms, atoms), jnp.int32),
        ],
        compiler_params=pltpu.CompilerParams(vmem_limit_bytes=SCOPE),
        name="forces",
    )(*map(inside, (lower, upper, probes, values, base, near)), positions, momenta, rate)


def move_beads(group, everyone, masses, table):
    _, _, _, local, atoms = everyone.shape
    return pl.pallas_call(
        bead_kernel,
        out_shape=(jax.ShapeDtypeStruct((3, local, atoms), F32),) * 2,
        in_specs=[SMEM_SPEC] + vmem(3),
        out_specs=tuple(vmem(2)),
        compiler_params=pltpu.CompilerParams(vmem_limit_bytes=SCOPE),
        name="bead_maps",
    )(group, inside(everyone), outside(masses), outside(table))


def body(
    positions, momenta, masses, features, neighbours, images, face_map,
    w_query, w_key, w_value, w_probe, radial_rate,
):
    groups = lax.axis_size("bead")
    beads = positions.shape[0]
    face_map, features, neighbours, images = map(outside, (face_map, features, neighbours, images))
    w_query, w_key, w_value, w_probe = map(outside, (w_query, w_key, w_value, w_probe))
    slabs = lax.axis_size("space")
    up = [(i, (i + 1) % slabs) for i in range(slabs)]
    down = [(target, source) for source, target in up]
    pos = outside(jnp.transpose(positions, (1, 0, 2)))
    mom = outside(jnp.transpose(momenta, (1, 0, 2)))
    radial_rate = outside(radial_rate[None])
    message = pack(features, pos, face_map)
    upper = lax.ppermute(message, "space", down)
    lower = lax.ppermute(message, "space", up)
    halo_free = own_slab(
        features, neighbours, images, pos, w_query, w_key, w_value, w_probe
    )
    sent = forces(groups, lower, upper, *halo_free, pos, mom, radial_rate)
    everyone = lax.all_to_all(sent, "bead", 0, 0, tiled=True)
    table = jnp.asarray(bead_maps(beads * groups, groups))
    group = lax.axis_index("bead").astype(jnp.int32)[None]
    new_pos, new_mom = move_beads(group, everyone, masses[None], table)
    return jnp.transpose(new_pos, (1, 0, 2)), jnp.transpose(new_mom, (1, 0, 2))


def solution(mesh):
    placed = (
        P("bead", None, "space"),
        P("bead", None, "space"),
        P("space"),
        P("bead", "space", None),
        P(None, "space"),
        P(None, "space"),
        P(None, "space", None),
        P(), P(), P(), P(), P(),
    )
    return jax.shard_map(
        body,
        mesh=mesh,
        in_specs=placed,
        out_specs=(P("bead", None, "space"), P("bead", None, "space")),
        check_vma=False,
    )
```
